32 devices in a mesh: ens: 4 (over x, core), state: 8 (over z, y).
Axes of the slice: x: 2, y: 2, z: 4, core: 2. Of those that a mesh axis runs over, the one named last changes fastest.
Arguments:
- ensemble: float32 [3072, 4096], P('state', 'ens'), may hold values from -18 to 18
- obs_values: float32 [2, 256], replicated, may hold values from -6 to 6
- obs_noise: bfloat16 [2, 256, 4096], P(None, None, 'ens'), may hold values from -6 to 6
- obs_var: float32 [2, 256], replicated, may hold values from 0.25 to 2
- obs_offset: int32 [2, 256], replicated, may hold values from 0 to 383, as said below
- owner: int32 [2], replicated, may hold values from 0 to 7
Outputs:
- analysis: float32 [3072, 4096], P('state', 'ens')
The draws below stay inside these ranges and needn't reach their ends.
Inputs may be any that keep to these rules, and one draw needn't show every extreme that they name: `obs_offset`: the 256 offsets of one batch are distinct.
All inputs are finite; a program needn't handle non-finite values.
Results may differ from the reference program's by a relative error of at most 0.0003.
Values sent between devices are 32-bit elements; how exact they have to be, the bound alone decides.
A program may use at most 64 MiB of HBM per device.

```python
import math
import jax
import jax.numpy as jnp
from jax import lax

S_DEV = 384
M_SUB = 1024
P_SIZE = 256
NB = 2
NS = 3072
M = 4096
LOC = 768
N_ENS = 4
N_STATE = 8


def draw_ensemble(key, part):
    key_centre = jax.random.fold_in(key, 11)
    key_scale = jax.random.fold_in(key, 12)
    key_member = jax.random.fold_in(key, 13)
    centre = jnp.clip(jax.random.normal(key_centre, (NS, 1), jnp.float32), -3.0, 3.0)
    scale = jnp.exp(jax.random.uniform(key_scale, (NS, 1), jnp.float32, jnp.log(0.3), jnp.log(3.0)))
    member = jnp.clip(jax.random.normal(key_member, (NS, M), jnp.float32), -5.0, 5.0)
    return (centre + scale * member).astype(jnp.float32)


def draw_obs_offset(key, part):
    batch_keys = jax.random.split(jax.random.fold_in(key, 21), NB)
    return jax.vmap(lambda single: jax.random.permutation(single, S_DEV)[:P_SIZE])(batch_keys).astype(jnp.int32)


def block_levels(rng, dims, cuts, low, top_value):
    def one(dim, shards_of):
        heights = jax.random.uniform(jax.random.fold_in(jax.random.fold_in(rng, 6), dim), (shards_of,), jnp.float32, low / len(cuts), top_value / len(cuts))
        return jnp.repeat(jnp.exp(heights), dims[dim] // shards_of).reshape((-1,) + (1,) * (len(dims) - dim - 1))

    level = one(*cuts[0])
    for cut in cuts[1:]:
        level = level * one(*cut)
    return level


def normal_values(key, dims, scale, most, cuts=(), held_as=jnp.bfloat16):
    array = scale * jax.random.normal(key, dims, jnp.float32)
    if cuts:
        array = array * block_levels(key, dims, cuts, -0.22, 0.18)
    return jnp.clip(array, -most, most).astype(held_as)


def setup_inputs(seed: int = 0) -> dict:
    streams_of = jax.random.split(jax.random.key(seed), 7)
    return {
        "ensemble": draw_ensemble(jax.random.fold_in(streams_of[6], 71), 0),
        "obs_values": normal_values(streams_of[1], (NB, P_SIZE), 1.0, 6.0, (), jnp.float32),
        "obs_noise": normal_values(streams_of[2], (NB, P_SIZE, M), 1.0, 6.0, ((2, 4),)),
        "obs_var": jnp.clip(jnp.exp(jax.random.uniform(streams_of[3], (NB, P_SIZE), jnp.float32, math.log(0.25), math.log(2.0))), 0.25, 2.0),
        "obs_offset": draw_obs_offset(jax.random.fold_in(streams_of[6], 71), 0),
        "owner": jax.random.randint(streams_of[5], (NB,), 0, N_STATE).astype(jnp.int32),
    }


finest = lax.Precision.HIGHEST

def cycle_taper(first, second, total, reach):
    distance = jnp.abs(first - second)
    distance = jnp.minimum(distance, total - distance).astype(jnp.float32)
    ratio = distance / jnp.float32(reach)
    return 1.0 / (1.0 + ratio * ratio)

def reference(ensemble, obs_values, obs_noise, obs_var, obs_offset, owner):
    states = S_DEV * N_STATE
    members = M_SUB * N_ENS
    current = ensemble
    for batch in range(NB):
        places = (owner[batch] * S_DEV + obs_offset[batch]).astype(jnp.int32)
        prior = current[places]
        obs_anom = prior - (lax.optimization_barrier(jnp.sum(prior, axis=1)) / members)[:, None]
        spread = jnp.einsum('pm,qm->pq', obs_anom, obs_anom, precision=finest)
        obs_cov = cycle_taper(places[:, None], places[None, :], states, LOC) * (spread / (members - 1)) + jnp.diag(obs_var[batch])
        factor = jnp.linalg.cholesky(obs_cov)
        variance = obs_var[batch]
        misfit = obs_values[batch][:, None] + jnp.sqrt(variance)[:, None] * obs_noise[batch].astype(jnp.float32) - prior
        solved = jax.scipy.linalg.cho_solve((factor, True), misfit)
        blocks = current.reshape(N_STATE, S_DEV, members)
        block_ids = jnp.arange(N_STATE, dtype=jnp.int32)

        def update(item_pair):
            block, block_id = item_pair
            positions = block_id * S_DEV + jnp.arange(S_DEV, dtype=jnp.int32)
            cross = jnp.einsum('sm,pm->sp', block, obs_anom, precision=finest)
            gain = cycle_taper(positions[:, None], places[None, :], states, LOC) * (cross / (members - 1))
            return block + jnp.dot(gain.astype(jnp.float32), solved.astype(jnp.float32), precision=finest, preferred_element_type=jnp.float32)
        current = lax.map(update, (blocks, block_ids)).reshape(states, members)
    return current
```

```python
import functools

import jax
import jax.numpy as jnp
from jax import lax
from jax.experimental import pallas as pl
from jax.experimental.pallas import tpu as pltpu
from jax.sharding import PartitionSpec as P

NB = 2
LAG = 3
CHUNKS = 16
SUM_CHUNKS = 4
MESH = pl.DeviceIdType.MESH
finest = lax.Precision.HIGHEST


def cycle_taper(first, second, total, reach):
    distance = jnp.abs(first - second)
    distance = jnp.minimum(distance, total - distance).astype(jnp.float32)
    ratio = distance / jnp.float32(reach)
    return 1.0 / (1.0 + ratio * ratio)


def spread_kernel(
    n_state, n_ens,
    own, sums, out, sums_out,
    right_in, left_in, right_out, left_out, total, side_in, ens_in, ens_total, state_in,
    right_send, right_recv, left_send, left_recv, side_send, side_recv,
    ens_send, ens_recv, state_send, state_recv,
):
    rows = own.shape[0] // CHUNKS
    here = lax.axis_index("state")
    ens = lax.axis_index("ens")
    last = n_state // 2 - 1
    place = here // 2
    side = here + 1 - 2 * lax.rem(here, 2)

    barrier = pltpu.get_barrier_semaphore()
    for step in range(1, n_ens):
        pl.semaphore_signal(
            barrier, inc=1, device_id={"ens": lax.rem(ens + step, n_ens)}, device_id_type=MESH
        )
    for step in range(1, n_state):
        pl.semaphore_signal(
            barrier, inc=1, device_id={"state": lax.rem(here + step, n_state)}, device_id_type=MESH
        )
    pl.semaphore_wait(barrier, n_ens + n_state - 2)

    def remote(src, dst, send, recv, target):
        return pltpu.make_async_remote_copy(
            src_ref=src, dst_ref=dst, send_sem=send, recv_sem=recv,
            device_id=target, device_id_type=MESH,
        )

    def ens_copy(step):
        return remote(
            sums, ens_in.at[step - 1], ens_send.at[step - 1], ens_recv.at[step - 1],
            {"ens": lax.rem(ens + step, n_ens)},
        )

    def state_copy(step):
        return remote(
            ens_total, state_in.at[step - 1], state_send.at[step - 1], state_recv.at[step - 1],
            {"state": lax.rem(here + step, n_state)},
        )

    def span(c):
        return pl.ds(pl.multiple_of(c * rows, rows), rows)

    def right_copy(src, c):
        return remote(
            src.at[span(c)], right_in.at[span(c)], right_send.at[c], right_recv.at[c],
            {"state": lax.rem(here + 2, n_state)},
        )

    def left_copy(src, c):
        return remote(
            src.at[span(c)], left_in.at[span(c)], left_send.at[c], left_recv.at[c],
            {"state": lax.rem(here + n_state - 2, n_state)},
        )

    def side_copy(c):
        return remote(
            total.at[span(c)], side_in.at[span(c)], side_send.at[c], side_recv.at[c],
            {"state": side},
        )

    def each(body):
        lax.fori_loop(0, CHUNKS, lambda c, carry: (body(c), carry)[1], 0)

    for step in range(1, n_ens):
        ens_copy(step).start()
    if last > 0:
        @pl.when(place == 0)
        def _():
            each(lambda c: right_copy(own, c).start())

        @pl.when(place == last)
        def _():
            each(lambda c: left_copy(own, c).start())

    for step in range(1, n_ens):
        ens_copy(step).wait_recv()
    whole = sums[...]
    for step in range(1, n_ens):
        whole = whole + ens_in[step - 1]
    ens_total[...] = whole
    for step in range(1, n_state):
        state_copy(step).start()

    def right_step(c):
        @pl.when(place > 0)
        def _():
            right_copy(own, c).wait_recv()
            right_out[span(c)] = own[span(c)] + right_in[span(c)]

            @pl.when(place < last)
            def _():
                right_copy(right_out, c).start()

    def left_step(c):
        @pl.when(place < last)
        def _():
            left_copy(own, c).wait_recv()
            left_out[span(c)] = own[span(c)] + left_in[span(c)]

            @pl.when(place > 0)
            def _():
                left_copy(left_out, c).start()

    def turn(t, carry):
        late = t - LAG

        @pl.when(t < CHUNKS)
        def _():
            @pl.when(2 * place <= last)
            def _():
                right_step(t)

            @pl.when(2 * place > last)
            def _():
                left_step(t)

        @pl.when(late >= 0)
        def _():
            @pl.when(2 * place <= last)
            def _():
                left_step(late)

            @pl.when(2 * place > last)
            def _():
                right_step(late)

            if last == 0:
                total[span(late)] = own[span(late)]
            else:
                @pl.when(place == 0)
                def _():
                    total[span(late)] = left_out[span(late)]

                @pl.when(place == last)
                def _():
                    total[span(late)] = right_out[span(late)]

                @pl.when((place > 0) & (place < last))
                def _():
                    total[span(late)] = right_out[span(late)] + left_in[span(late)]

            side_copy(late).start()

        return carry

    lax.fori_loop(0, CHUNKS + LAG, turn, 0)

    def finish(c):
        side_copy(c).wait_recv()
        out[span(c)] = total[span(c)] + side_in[span(c)]

    each(finish)
    for step in range(1, n_state):
        state_copy(step).wait_recv()
    whole = ens_total[...]
    for step in range(1, n_state):
        whole = whole + state_in[step - 1]
    sums_out[...] = whole

    for step in range(1, n_ens):
        ens_copy(step).wait_send()
    for step in range(1, n_state):
        state_copy(step).wait_send()
    each(lambda c: side_copy(c).wait_send())

    @pl.when(place < last)
    def _():
        each(lambda c: right_copy(own, c).wait_send())

    @pl.when(place > 0)
    def _():
        each(lambda c: left_copy(own, c).wait_send())


def spread_call(n_state, n_ens, own, sums):
    vmem = pl.BlockSpec(memory_space=pltpu.VMEM)
    big = pltpu.VMEM(own.shape, own.dtype)
    dma = pltpu.SemaphoreType.DMA
    return pl.pallas_call(
        functools.partial(spread_kernel, n_state, n_ens),
        out_shape=(
            jax.ShapeDtypeStruct(own.shape, own.dtype),
            jax.ShapeDtypeStruct(sums.shape, sums.dtype),
        ),
        in_specs=[vmem] * 2,
        out_specs=(vmem, vmem),
        scratch_shapes=[big] * 6
        + [
            pltpu.VMEM((n_ens - 1,) + sums.shape, sums.dtype),
            pltpu.VMEM(sums.shape, sums.dtype),
            pltpu.VMEM((n_state - 1,) + sums.shape, sums.dtype),
        ]
        + [dma((CHUNKS,))] * 6
        + [dma((n_ens - 1,))] * 2
        + [dma((n_state - 1,))] * 2,
        compiler_params=pltpu.CompilerParams(
            collective_id=0, has_side_effects=True, vmem_limit_bytes=40 * 2**20
        ),
        name="spread",
    )(own, sums)


def sum_kernel(n_ens, part, out, pair_in, step_out, step_in, back_out, back_in, *sems):
    half = part.shape[0] // 2
    rows = half // SUM_CHUNKS
    ens = lax.axis_index("ens")
    low = lax.rem(ens, 2)
    bits = [1]
    while bits[-1] * 2 < n_ens:
        bits.append(bits[-1] * 2)

    def partner(bit):
        return {"ens": ens + bit - 2 * bit * lax.rem(ens // bit, 2)}

    barrier = pltpu.get_barrier_semaphore()
    for bit in bits:
        pl.semaphore_signal(barrier, inc=1, device_id=partner(bit), device_id_type=MESH)
    pl.semaphore_wait(barrier, len(bits))

    def remote(src, dst, which, c, bit):
        return pltpu.make_async_remote_copy(
            src_ref=src, dst_ref=dst,
            send_sem=sems[which].at[0, c], recv_sem=sems[which].at[1, c],
            device_id=partner(bit), device_id_type=MESH,
        )

    def span(c, base=0):
        return pl.ds(pl.multiple_of(base * half + c * rows, rows), rows)

    def pair_copy(c):
        return remote(part.at[span(c, 1 - low)], pair_in.at[span(c)], 0, c, 1)

    def step_copy(i, c):
        return remote(step_out.at[i, span(c)], step_in.at[i, span(c)], 2 + i, c, bits[i + 1])

    def back_copy(c):
        return remote(back_out.at[span(c)], back_in.at[span(c)], 1, c, 1)

    steps = len(bits) - 1
    for c in range(SUM_CHUNKS):
        pair_copy(c).start()
    for c in range(SUM_CHUNKS):
        pair_copy(c).wait_recv()
        value = part[span(c, low)] + pair_in[span(c)]
        if steps:
            step_out[0, span(c)] = value
            step_copy(0, c).start()
        else:
            back_out[span(c)] = value
            back_copy(c).start()
    for i in range(steps):
        for c in range(SUM_CHUNKS):
            step_copy(i, c).wait_recv()
            value = step_out[i, span(c)] + step_in[i, span(c)]
            if i + 1 < steps:
                step_out[i + 1, span(c)] = value
                step_copy(i + 1, c).start()
            else:
                back_out[span(c)] = value
                back_copy(c).start()
    for c in range(SUM_CHUNKS):
        out[span(c, low)] = back_out[span(c)]
    for c in range(SUM_CHUNKS):
        back_copy(c).wait_recv()
        out[span(c, 1 - low)] = back_in[span(c)]
    for c in range(SUM_CHUNKS):
        pair_copy(c).wait_send()
        back_copy(c).wait_send()
        for i in range(steps):
            step_copy(i, c).wait_send()


def sum_call(n_ens, part):
    vmem = pl.BlockSpec(memory_space=pltpu.VMEM)
    half = (part.shape[0] // 2, part.shape[1])
    steps = max(1, (n_ens - 1).bit_length() - 1)
    dma = pltpu.SemaphoreType.DMA
    return pl.pallas_call(
        functools.partial(sum_kernel, n_ens),
        out_shape=jax.ShapeDtypeStruct(part.shape, part.dtype),
        in_specs=[vmem],
        out_specs=vmem,
        scratch_shapes=[
            pltpu.VMEM(half, part.dtype),
            pltpu.VMEM((steps,) + half, part.dtype),
            pltpu.VMEM((steps,) + half, part.dtype),
            pltpu.VMEM(half, part.dtype),
            pltpu.VMEM(half, part.dtype),
        ]
        + [dma((2, SUM_CHUNKS))] * (2 + steps),
        compiler_params=pltpu.CompilerParams(
            collective_id=1, has_side_effects=True, vmem_limit_bytes=32 * 2**20
        ),
        name="ens_sum",
    )(part)


def mul(a, b):
    return jnp.dot(a, b, precision=finest, preferred_element_type=jnp.float32)


def invert(a):
    size = a.shape[0]
    across = lax.broadcasted_iota(jnp.int32, (1, size), 1)
    down = lax.broadcasted_iota(jnp.int32, (size, 1), 0)
    for k in range(size):
        column = a[:, k : k + 1]
        pivot = 1.0 / a[k : k + 1, k : k + 1]
        row = jnp.where(across == k, 1.0, a[k : k + 1, :]) * pivot
        rest = jnp.where(across == k, 0.0, a) - column * row
        a = jnp.where(down == k, row, rest)
    return a


def solve_kernel(moments, scale, diagonal, out):
    size = moments.shape[0]
    half = size // 2
    cov = moments[:, :size] * scale[:, :size] + diagonal[...]
    right = moments[:, size:] * scale[:, size:]
    corner = invert(cov[:half, :half])
    cross = cov[:half, half:]
    across = mul(corner, cross)
    rest = invert(cov[half:, half:] - mul(cross.T, across))
    first = mul(corner, right[:half])
    second = mul(rest, right[half:] - mul(cross.T, first))
    out[half:] = second
    out[:half] = first - mul(across, second)


def solve_call(moments, scale, diagonal):
    vmem = pl.BlockSpec(memory_space=pltpu.VMEM)
    size = moments.shape[0]
    return pl.pallas_call(
        solve_kernel,
        out_shape=jax.ShapeDtypeStruct((size, moments.shape[1] - size), jnp.float32),
        in_specs=[vmem] * 3,
        out_specs=vmem,
        compiler_params=pltpu.CompilerParams(vmem_limit_bytes=32 * 2**20),
        name="gain",
    )(moments, scale, diagonal)


def local(ensemble, obs_values, obs_noise, obs_var, obs_offset, owner):
    rows, width = ensemble.shape
    n_ens = lax.axis_size("ens")
    n_state = lax.axis_size("state")
    members = width * n_ens
    states = rows * n_state
    reach = states // 4
    here = lax.axis_index("state")
    positions = here * rows + jnp.arange(rows, dtype=jnp.int32)
    current = ensemble
    for batch in range(NB):
        places = owner[batch] * rows + obs_offset[batch]
        aims = jnp.concatenate([places, positions])
        scale = cycle_taper(places[:, None], aims[None, :], states, reach) / (members - 1)
        diagonal = jnp.diag(obs_var[batch])
        local_rows = jnp.take(current, obs_offset[batch], axis=0)
        masked = jnp.where(here == owner[batch], local_rows, 0.0)
        sums = jnp.broadcast_to(jnp.sum(masked, axis=1)[None, :], (8, masked.shape[0]))
        prior, totals = spread_call(n_state, n_ens, masked, sums)
        anom = prior - (totals[0] / members)[:, None]
        spread = jnp.einsum("pm,qm->pq", anom, anom, precision=finest)
        cross = jnp.einsum("pm,sm->ps", anom, current, precision=finest)
        moments = sum_call(n_ens, jnp.concatenate([spread, cross], axis=1))
        gain = solve_call(moments, scale, diagonal)
        variance = obs_var[batch]
        misfit = (
            obs_values[batch][:, None]
            + jnp.sqrt(variance)[:, None] * obs_noise[batch].astype(jnp.float32)
            - prior
        )
        current = current + jnp.einsum("ps,pm->sm", gain, misfit, precision=finest)
    return current


def solution(mesh):
    in_specs = (P("state", "ens"), P(), P(None, None, "ens"), P(), P(), P())
    out_specs = P("state", "ens")
    return jax.shard_map(local, mesh=mesh, in_specs=in_specs, out_specs=out_specs, check_vma=False)
```

```python
import functools

import jax
import jax.numpy as jnp
from jax import lax
from jax.experimental import pallas as pl
from jax.experimental.pallas import tpu as pltpu
from jax.sharding import PartitionSpec as P

NB = 2
LAG = 3
CHUNKS = 32
SUM_CHUNKS = 4
MESH = pl.DeviceIdType.MESH
finest = lax.Precision.HIGHEST


def cycle_taper(first, second, total, reach):
    distance = jnp.abs(first - second)
    distance = jnp.minimum(distance, total - distance).astype(jnp.float32)
    ratio = distance / jnp.float32(reach)
    return 1.0 / (1.0 + ratio * ratio)


def spread_kernel(
    n_state, n_ens,
    own, sums, out, sums_out,
    right_in, left_in, right_out, left_out, total, side_in, ens_in, ens_total, state_in,
    right_send, right_recv, left_send, left_recv, side_send, side_recv,
    ens_send, ens_recv, state_send, state_recv,
):
    rows = own.shape[0] // CHUNKS
    here = lax.axis_index("state")
    ens = lax.axis_index("ens")
    last = n_state // 2 - 1
    place = here // 2
    side = here + 1 - 2 * lax.rem(here, 2)

    barrier = pltpu.get_barrier_semaphore()
    for step in range(1, n_ens):
        pl.semaphore_signal(
            barrier, inc=1, device_id={"ens": lax.rem(ens + step, n_ens)}, device_id_type=MESH
        )
    for step in range(1, n_state):
        pl.semaphore_signal(
            barrier, inc=1, device_id={"state": lax.rem(here + step, n_state)}, device_id_type=MESH
        )
    pl.semaphore_wait(barrier, n_ens + n_state - 2)

    def remote(src, dst, send, recv, target):
        return pltpu.make_async_remote_copy(
            src_ref=src, dst_ref=dst, send_sem=send, recv_sem=recv,
            device_id=target, device_id_type=MESH,
        )

    def ens_copy(step):
        return remote(
            sums, ens_in.at[step - 1], ens_send.at[step - 1], ens_recv.at[step - 1],
            {"ens": lax.rem(ens + step, n_ens)},
        )

    def state_copy(step):
        return remote(
            ens_total, state_in.at[step - 1], state_send.at[step - 1], state_recv.at[step - 1],
            {"state": lax.rem(here + step, n_state)},
        )

    def span(c):
        return pl.ds(pl.multiple_of(c * rows, rows), rows)

    def right_copy(src, c):
        return remote(
            src.at[span(c)], right_in.at[span(c)], right_send.at[c], right_recv.at[c],
            {"state": lax.rem(here + 2, n_state)},
        )

    def left_copy(src, c):
        return remote(
            src.at[span(c)], left_in.at[span(c)], left_send.at[c], left_recv.at[c],
            {"state": lax.rem(here + n_state - 2, n_state)},
        )

    def side_copy(c):
        return remote(
            total.at[span(c)], side_in.at[span(c)], side_send.at[c], side_recv.at[c],
            {"state": side},
        )

    def each(body):
        lax.fori_loop(0, CHUNKS, lambda c, carry: (body(c), carry)[1], 0)

    for step in range(1, n_ens):
        ens_copy(step).start()
    if last > 0:
        @pl.when(place == 0)
        def _():
            each(lambda c: right_copy(own, c).start())

        @pl.when(place == last)
        def _():
            each(lambda c: left_copy(own, c).start())

    for step in range(1, n_ens):
        ens_copy(step).wait_recv()
    whole = sums[...]
    for step in range(1, n_ens):
        whole = whole + ens_in[step - 1]
    ens_total[...] = whole
    for step in range(1, n_state):
        state_copy(step).start()

    def right_step(c):
        @pl.when(place > 0)
        def _():
            right_copy(own, c).wait_recv()
            right_out[span(c)] = own[span(c)] + right_in[span(c)]

            @pl.when(place < last)
            def _():
                right_copy(right_out, c).start()

    def left_step(c):
        @pl.when(place < last)
        def _():
            left_copy(own, c).wait_recv()
            left_out[span(c)] = own[span(c)] + left_in[span(c)]

            @pl.when(place > 0)
            def _():
                left_copy(left_out, c).start()

    def turn(t, carry):
        late = t - LAG

        @pl.when(t < CHUNKS)
        def _():
            @pl.when(2 * place <= last)
            def _():
                right_step(t)

            @pl.when(2 * place > last)
            def _():
                left_step(t)

        @pl.when(late >= 0)
        def _():
            @pl.when(2 * place <= last)
            def _():
                left_step(late)

            @pl.when(2 * place > last)
            def _():
                right_step(late)

            if last == 0:
                total[span(late)] = own[span(late)]
            else:
                @pl.when(place == 0)
                def _():
                    total[span(late)] = left_out[span(late)]

                @pl.when(place == last)
                def _():
                    total[span(late)] = right_out[span(late)]

                @pl.when((place > 0) & (place < last))
                def _():
                    total[span(late)] = right_out[span(late)] + left_in[span(late)]

            side_copy(late).start()

        return carry

    lax.fori_loop(0, CHUNKS + LAG, turn, 0)

    def finish(c):
        side_copy(c).wait_recv()
        out[span(c)] = total[span(c)] + side_in[span(c)]

    each(finish)
    for step in range(1, n_state):
        state_copy(step).wait_recv()
    whole = ens_total[...]
    for step in range(1, n_state):
        whole = whole + state_in[step - 1]
    sums_out[...] = whole

    for step in range(1, n_ens):
        ens_copy(step).wait_send()
    for step in range(1, n_state):
        state_copy(step).wait_send()
    each(lambda c: side_copy(c).wait_send())

    @pl.when(place < last)
    def _():
        each(lambda c: right_copy(own, c).wait_send())

    @pl.when(place > 0)
    def _():
        each(lambda c: left_copy(own, c).wait_send())


def spread_call(n_state, n_ens, own, sums):
    vmem = pl.BlockSpec(memory_space=pltpu.VMEM)
    big = pltpu.VMEM(own.shape, own.dtype)
    dma = pltpu.SemaphoreType.DMA
    return pl.pallas_call(
        functools.partial(spread_kernel, n_state, n_ens),
        out_shape=(
            jax.ShapeDtypeStruct(own.shape, own.dtype),
            jax.ShapeDtypeStruct(sums.shape, sums.dtype),
        ),
        in_specs=[vmem] * 2,
        out_specs=(vmem, vmem),
        scratch_shapes=[big] * 6
        + [
            pltpu.VMEM((n_ens - 1,) + sums.shape, sums.dtype),
            pltpu.VMEM(sums.shape, sums.dtype),
            pltpu.VMEM((n_state - 1,) + sums.shape, sums.dtype),
        ]
        + [dma((CHUNKS,))] * 6
        + [dma((n_ens - 1,))] * 2
        + [dma((n_state - 1,))] * 2,
        compiler_params=pltpu.CompilerParams(
            collective_id=0, has_side_effects=True, vmem_limit_bytes=40 * 2**20
        ),
        name="spread",
    )(own, sums)


def sum_kernel(n_ens, part, out, pair_in, step_out, step_in, back_out, back_in, *sems):
    half = part.shape[0] // 2
    rows = half // SUM_CHUNKS
    ens = lax.axis_index("ens")
    low = lax.rem(ens, 2)
    bits = [1]
    while bits[-1] * 2 < n_ens:
        bits.append(bits[-1] * 2)

    def partner(bit):
        return {"ens": ens + bit - 2 * bit * lax.rem(ens // bit, 2)}

    barrier = pltpu.get_barrier_semaphore()
    for bit in bits:
        pl.semaphore_signal(barrier, inc=1, device_id=partner(bit), device_id_type=MESH)
    pl.semaphore_wait(barrier, len(bits))

    def remote(src, dst, which, c, bit):
        return pltpu.make_async_remote_copy(
            src_ref=src, dst_ref=dst,
            send_sem=sems[which].at[0, c], recv_sem=sems[which].at[1, c],
            device_id=partner(bit), device_id_type=MESH,
        )

    def span(c, base=0):
        return pl.ds(pl.multiple_of(base * half + c * rows, rows), rows)

    def pair_copy(c):
        return remote(part.at[span(c, 1 - low)], pair_in.at[span(c)], 0, c, 1)

    def step_copy(i, c):
        return remote(step_out.at[i, span(c)], step_in.at[i, span(c)], 2 + i, c, bits[i + 1])

    def back_copy(c):
        return remote(back_out.at[span(c)], back_in.at[span(c)], 1, c, 1)

    steps = len(bits) - 1
    for c in range(SUM_CHUNKS):
        pair_copy(c).start()
    for c in range(SUM_CHUNKS):
        pair_copy(c).wait_recv()
        value = part[span(c, low)] + pair_in[span(c)]
        if steps:
            step_out[0, span(c)] = value
            step_copy(0, c).start()
        else:
            back_out[span(c)] = value
            back_copy(c).start()
    for i in range(steps):
        for c in range(SUM_CHUNKS):
            step_copy(i, c).wait_recv()
            value = step_out[i, span(c)] + step_in[i, span(c)]
            if i + 1 < steps:
                step_out[i + 1, span(c)] = value
                step_copy(i + 1, c).start()
            else:
                back_out[span(c)] = value
                back_copy(c).start()
    for c in range(SUM_CHUNKS):
        out[span(c, low)] = back_out[span(c)]
    for c in range(SUM_CHUNKS):
        back_copy(c).wait_recv()
        out[span(c, 1 - low)] = back_in[span(c)]
    for c in range(SUM_CHUNKS):
        pair_copy(c).wait_send()
        back_copy(c).wait_send()
        for i in range(steps):
            step_copy(i, c).wait_send()


def sum_call(n_ens, part, ident):
    vmem = pl.BlockSpec(memory_space=pltpu.VMEM)
    half = (part.shape[0] // 2, part.shape[1])
    steps = max(1, (n_ens - 1).bit_length() - 1)
    dma = pltpu.SemaphoreType.DMA
    return pl.pallas_call(
        functools.partial(sum_kernel, n_ens),
        out_shape=jax.ShapeDtypeStruct(part.shape, part.dtype),
        in_specs=[vmem],
        out_specs=vmem,
        scratch_shapes=[
            pltpu.VMEM(half, part.dtype),
            pltpu.VMEM((steps,) + half, part.dtype),
            pltpu.VMEM((steps,) + half, part.dtype),
            pltpu.VMEM(half, part.dtype),
            pltpu.VMEM(half, part.dtype),
        ]
        + [dma((2, SUM_CHUNKS))] * (2 + steps),
        compiler_params=pltpu.CompilerParams(
            collective_id=ident, has_side_effects=True, vmem_limit_bytes=32 * 2**20
        ),
        name="ens_sum",
    )(part)


def mul(a, b):
    return jnp.dot(a, b, precision=finest, preferred_element_type=jnp.float32)


def invert(a):
    size = a.shape[0]
    across = lax.broadcasted_iota(jnp.int32, (8, size), 1)
    down = lax.broadcasted_iota(jnp.int32, (8, size), 0)
    blocks = [a[8 * i : 8 * i + 8, :] for i in range(size // 8)]
    for k in range(len(blocks)):
        base = 8 * k
        panel = blocks[k]
        columns = [
            jnp.broadcast_to(panel[:, base + j : base + j + 1], (8, size)) for j in range(8)
        ]
        for j in range(8):
            pivot = 1.0 / columns[j][j : j + 1, :]
            lead = columns[j]
            for i in range(8):
                if i != j:
                    entry = columns[i][j : j + 1, :] * pivot
                    columns[i] = jnp.where(down == j, entry, columns[i] - lead * entry)
            columns[j] = jnp.where(down == j, pivot, -lead * pivot)
        inside = (across >= base) & (across < base + 8)
        panel = jnp.where(inside, jnp.where(across - base == down, 1.0, 0.0), panel)
        terms = [columns[j] * panel[j : j + 1, :] for j in range(8)]
        while len(terms) > 1:
            terms = [terms[i] + terms[i + 1] for i in range(0, len(terms), 2)]
        panel = terms[0]
        order = list(range(k + 1, len(blocks))) + list(range(k))
        for i in order:
            block = blocks[i]
            terms = [block[:, base + j : base + j + 1] * panel[j : j + 1, :] for j in range(8)]
            while len(terms) > 1:
                terms = [terms[m] + terms[m + 1] for m in range(0, len(terms), 2)]
            blocks[i] = jnp.where(inside, 0.0, block) - terms[0]
        blocks[k] = panel
    return jnp.concatenate(blocks, axis=0)


def solve_kernel(moments, scale, diagonal, out):
    size = moments.shape[0]
    half = size // 2
    cov = moments[:, :size] * scale[:, :size] + diagonal[...]
    right = moments[:, size:] * scale[:, size:]
    corner = invert(cov[:half, :half])
    cross = cov[:half, half:]
    across = mul(corner, cross)
    rest = invert(cov[half:, half:] - mul(cross.T, across))
    first = mul(corner, right[:half])
    second = mul(rest, right[half:] - mul(cross.T, first))
    out[half:] = second
    out[:half] = first - mul(across, second)


def solve_call(moments, scale, diagonal):
    vmem = pl.BlockSpec(memory_space=pltpu.VMEM)
    size = moments.shape[0]
    return pl.pallas_call(
        solve_kernel,
        out_shape=jax.ShapeDtypeStruct((size, moments.shape[1] - size), jnp.float32),
        in_specs=[vmem] * 3,
        out_specs=vmem,
        compiler_params=pltpu.CompilerParams(vmem_limit_bytes=32 * 2**20),
        name="gain",
    )(moments, scale, diagonal)


def local(ensemble, obs_values, obs_noise, obs_var, obs_offset, owner):
    rows, width = ensemble.shape
    n_ens = lax.axis_size("ens")
    n_state = lax.axis_size("state")
    members = width * n_ens
    states = rows * n_state
    reach = states // 4
    size = obs_offset.shape[1]
    here = lax.axis_index("state")
    positions = here * rows + jnp.arange(rows, dtype=jnp.int32)
    places = owner[:, None] * rows + obs_offset

    masked = jnp.where(
        jnp.repeat(here == owner, size)[:, None],
        jnp.take(ensemble, obs_offset.reshape(-1), axis=0),
        0.0,
    )
    noise_sums = jnp.sum(obs_noise[: NB - 1].astype(jnp.float32), axis=2).reshape(-1)
    sums = jnp.concatenate([jnp.sum(masked, axis=1), jnp.where(here == 0, noise_sums, 0.0)])
    prior, totals = spread_call(n_state, n_ens, masked, jnp.broadcast_to(sums, (8,) + sums.shape))
    means = totals[0] / members
    noise_means = means[NB * size :].reshape(NB - 1, size)
    means = means[: NB * size].reshape(NB, size)
    current = jnp.concatenate([prior, ensemble], axis=0)
    aims = jnp.concatenate([places.reshape(-1), positions])
    for batch in range(NB):
        scale = cycle_taper(places[batch][:, None], aims[None, :], states, reach) / (members - 1)
        variance = obs_var[batch]
        prior, current, aims = current[:size], current[size:], aims[size:]
        anom = prior - means[0][:, None]
        spread = jnp.einsum("pm,qm->pq", anom, anom, precision=finest)
        cross = jnp.einsum("pm,sm->ps", anom, current, precision=finest)
        moments = sum_call(n_ens, jnp.concatenate([spread, cross], axis=1), 1 + batch)
        gain = solve_call(moments, scale, jnp.diag(variance))
        misfit = (
            obs_values[batch][:, None]
            + jnp.sqrt(variance)[:, None] * obs_noise[batch].astype(jnp.float32)
            - prior
        )
        current = current + jnp.einsum("ps,pm->sm", gain, misfit, precision=finest)
        if batch + 1 < NB:
            misfit_mean = obs_values[batch] + jnp.sqrt(variance) * noise_means[batch] - means[0]
            later = gain[:, : (NB - 1 - batch) * size]
            means = means[1:] + jnp.einsum(
                "ps,p->s", later, misfit_mean, precision=finest
            ).reshape(-1, size)
    return current


def solution(mesh):
    in_specs = (P("state", "ens"), P(), P(None, None, "ens"), P(), P(), P())
    out_specs = P("state", "ens")
    return jax.shard_map(local, mesh=mesh, in_specs=in_specs, out_specs=out_specs, check_vma=False)
```

```python
import functools

import jax
import jax.numpy as jnp
from jax import lax
from jax.experimental import pallas as pl
from jax.experimental.pallas import tpu as pltpu
from jax.sharding import PartitionSpec as P

NB = 2
LAG = 4
CHUNKS = 64
SUM_CHUNKS = 8
MESH = pl.DeviceIdType.MESH
finest = lax.Precision.HIGHEST


def cycle_taper(first, second, total, reach):
    distance = jnp.abs(first - second)
    distance = jnp.minimum(distance, total - distance).astype(jnp.float32)
    ratio = distance / jnp.float32(reach)
    return 1.0 / (1.0 + ratio * ratio)


def spread_kernel(
    n_state, n_ens,
    own, sums, out, sums_out,
    right_in, left_in, right_out, left_out, total, side_in, ens_in, ens_total, state_in,
    right_send, right_recv, left_send, left_recv, side_send, side_recv,
    ens_send, ens_recv, state_send, state_recv,
):
    rows = own.shape[0] // CHUNKS
    here = lax.axis_index("state")
    ens = lax.axis_index("ens")
    last = n_state // 2 - 1
    place = here // 2
    side = here + 1 - 2 * lax.rem(here, 2)

    barrier = pltpu.get_barrier_semaphore()
    for step in range(1, n_ens):
        pl.semaphore_signal(
            barrier, inc=1, device_id={"ens": lax.rem(ens + step, n_ens)}, device_id_type=MESH
        )
    for step in range(1, n_state):
        pl.semaphore_signal(
            barrier, inc=1, device_id={"state": lax.rem(here + step, n_state)}, device_id_type=MESH
        )
    pl.semaphore_wait(barrier, n_ens + n_state - 2)

    def remote(src, dst, send, recv, target):
        return pltpu.make_async_remote_copy(
            src_ref=src, dst_ref=dst, send_sem=send, recv_sem=recv,
            device_id=target, device_id_type=MESH,
        )

    def ens_copy(step):
        return remote(
            sums, ens_in.at[step - 1], ens_send.at[step - 1], ens_recv.at[step - 1],
            {"ens": lax.rem(ens + step, n_ens)},
        )

    def state_copy(step):
        return remote(
            ens_total, state_in.at[step - 1], state_send.at[step - 1], state_recv.at[step - 1],
            {"state": lax.rem(here + step, n_state)},
        )

    def span(c):
        return pl.ds(pl.multiple_of(c * rows, rows), rows)

    def right_copy(src, c):
        return remote(
            src.at[span(c)], right_in.at[span(c)], right_send.at[c], right_recv.at[c],
            {"state": lax.rem(here + 2, n_state)},
        )

    def left_copy(src, c):
        return remote(
            src.at[span(c)], left_in.at[span(c)], left_send.at[c], left_recv.at[c],
            {"state": lax.rem(here + n_state - 2, n_state)},
        )

    def side_copy(c):
        return remote(
            total.at[span(c)], side_in.at[span(c)], side_send.at[c], side_recv.at[c],
            {"state": side},
        )

    def each(body):
        lax.fori_loop(0, CHUNKS, lambda c, carry: (body(c), carry)[1], 0)

    for step in range(1, n_ens):
        ens_copy(step).start()
    if last > 0:
        @pl.when(place == 0)
        def _():
            each(lambda c: right_copy(own, c).start())

        @pl.when(place == last)
        def _():
            each(lambda c: left_copy(own, c).start())

    for step in range(1, n_ens):
        ens_copy(step).wait_recv()
    whole = sums[...]
    for step in range(1, n_ens):
        whole = whole + ens_in[step - 1]
    ens_total[...] = whole
    for step in range(1, n_state):
        state_copy(step).start()

    def right_step(c):
        @pl.when(place > 0)
        def _():
            right_copy(own, c).wait_recv()
            right_out[span(c)] = own[span(c)] + right_in[span(c)]

            @pl.when(place < last)
            def _():
                right_copy(right_out, c).start()

    def left_step(c):
        @pl.when(place < last)
        def _():
            left_copy(own, c).wait_recv()
            left_out[span(c)] = own[span(c)] + left_in[span(c)]

            @pl.when(place > 0)
            def _():
                left_copy(left_out, c).start()

    def turn(t, carry):
        late = t - LAG

        @pl.when(t < CHUNKS)
        def _():
            @pl.when(2 * place <= last)
            def _():
                right_step(t)

            @pl.when(2 * place > last)
            def _():
                left_step(t)

        @pl.when(late >= 0)
        def _():
            @pl.when(2 * place <= last)
            def _():
                left_step(late)

            @pl.when(2 * place > last)
            def _():
                right_step(late)

            if last == 0:
                total[span(late)] = own[span(late)]
            else:
                @pl.when(place == 0)
                def _():
                    total[span(late)] = left_out[span(late)]

                @pl.when(place == last)
                def _():
                    total[span(late)] = right_out[span(late)]

                @pl.when((place > 0) & (place < last))
                def _():
                    total[span(late)] = right_out[span(late)] + left_in[span(late)]

            side_copy(late).start()

        return carry

    lax.fori_loop(0, CHUNKS + LAG, turn, 0)

    def finish(c):
        side_copy(c).wait_recv()
        out[span(c)] = total[span(c)] + side_in[span(c)]

    each(finish)
    for step in range(1, n_state):
        state_copy(step).wait_recv()
    whole = ens_total[...]
    for step in range(1, n_state):
        whole = whole + state_in[step - 1]
    sums_out[...] = whole

    for step in range(1, n_ens):
        ens_copy(step).wait_send()
    for step in range(1, n_state):
        state_copy(step).wait_send()
    each(lambda c: side_copy(c).wait_send())

    @pl.when(place < last)
    def _():
        each(lambda c: right_copy(own, c).wait_send())

    @pl.when(place > 0)
    def _():
        each(lambda c: left_copy(own, c).wait_send())


def spread_call(n_state, n_ens, own, sums):
    vmem = pl.BlockSpec(memory_space=pltpu.VMEM)
    big = pltpu.VMEM(own.shape, own.dtype)
    dma = pltpu.SemaphoreType.DMA
    return pl.pallas_call(
        functools.partial(spread_kernel, n_state, n_ens),
        out_shape=(
            jax.ShapeDtypeStruct(own.shape, own.dtype),
            jax.ShapeDtypeStruct(sums.shape, sums.dtype),
        ),
        in_specs=[vmem] * 2,
        out_specs=(vmem, vmem),
        scratch_shapes=[big] * 6
        + [
            pltpu.VMEM((n_ens - 1,) + sums.shape, sums.dtype),
            pltpu.VMEM(sums.shape, sums.dtype),
            pltpu.VMEM((n_state - 1,) + sums.shape, sums.dtype),
        ]
        + [dma((CHUNKS,))] * 6
        + [dma((n_ens - 1,))] * 2
        + [dma((n_state - 1,))] * 2,
        compiler_params=pltpu.CompilerParams(
            collective_id=0, has_side_effects=True, vmem_limit_bytes=40 * 2**20
        ),
        name="spread",
    )(own, sums)


def sum_kernel(n_ens, part, out, pair_in, step_out, step_in, back_out, back_in, *sems):
    half = part.shape[0] // 2
    rows = half // SUM_CHUNKS
    ens = lax.axis_index("ens")
    low = lax.rem(ens, 2)
    bits = [1]
    while bits[-1] * 2 < n_ens:
        bits.append(bits[-1] * 2)

    def partner(bit):
        return {"ens": ens + bit - 2 * bit * lax.rem(ens // bit, 2)}

    barrier = pltpu.get_barrier_semaphore()
    for bit in bits:
        pl.semaphore_signal(barrier, inc=1, device_id=partner(bit), device_id_type=MESH)
    pl.semaphore_wait(barrier, len(bits))

    def remote(src, dst, which, c, bit):
        return pltpu.make_async_remote_copy(
            src_ref=src, dst_ref=dst,
            send_sem=sems[which].at[0, c], recv_sem=sems[which].at[1, c],
            device_id=partner(bit), device_id_type=MESH,
        )

    def span(c, base=0):
        return pl.ds(pl.multiple_of(base * half + c * rows, rows), rows)

    def pair_copy(c):
        return remote(part.at[span(c, 1 - low)], pair_in.at[span(c)], 0, c, 1)

    def step_copy(i, c):
        return remote(step_out.at[i, span(c)], step_in.at[i, span(c)], 2 + i, c, bits[i + 1])

    def back_copy(c):
        return remote(back_out.at[span(c)], back_in.at[span(c)], 1, c, 1)

    steps = len(bits) - 1
    for c in range(SUM_CHUNKS):
        pair_copy(c).start()
    for c in range(SUM_CHUNKS):
        pair_copy(c).wait_recv()
        value = part[span(c, low)] + pair_in[span(c)]
        if steps:
            step_out[0, span(c)] = value
            step_copy(0, c).start()
        else:
            back_out[span(c)] = value
            back_copy(c).start()
    for i in range(steps):
        for c in range(SUM_CHUNKS):
            step_copy(i, c).wait_recv()
            value = step_out[i, span(c)] + step_in[i, span(c)]
            if i + 1 < steps:
                step_out[i + 1, span(c)] = value
                step_copy(i + 1, c).start()
            else:
                back_out[span(c)] = value
                back_copy(c).start()
    for c in range(SUM_CHUNKS):
        out[span(c, low)] = back_out[span(c)]
    for c in range(SUM_CHUNKS):
        back_copy(c).wait_recv()
        out[span(c, 1 - low)] = back_in[span(c)]
    for c in range(SUM_CHUNKS):
        pair_copy(c).wait_send()
        back_copy(c).wait_send()
        for i in range(steps):
            step_copy(i, c).wait_send()


def sum_call(n_ens, part, ident):
    vmem = pl.BlockSpec(memory_space=pltpu.VMEM)
    half = (part.shape[0] // 2, part.shape[1])
    steps = max(1, (n_ens - 1).bit_length() - 1)
    dma = pltpu.SemaphoreType.DMA
    return pl.pallas_call(
        functools.partial(sum_kernel, n_ens),
        out_shape=jax.ShapeDtypeStruct(part.shape, part.dtype),
        in_specs=[vmem],
        out_specs=vmem,
        scratch_shapes=[
            pltpu.VMEM(half, part.dtype),
            pltpu.VMEM((steps,) + half, part.dtype),
            pltpu.VMEM((steps,) + half, part.dtype),
            pltpu.VMEM(half, part.dtype),
            pltpu.VMEM(half, part.dtype),
        ]
        + [dma((2, SUM_CHUNKS))] * (2 + steps),
        compiler_params=pltpu.CompilerParams(
            collective_id=ident, has_side_effects=True, vmem_limit_bytes=32 * 2**20
        ),
        name="ens_sum",
    )(part)


def mul(a, b):
    return jnp.dot(a, b, precision=finest, preferred_element_type=jnp.float32)


def invert(a):
    size = a.shape[0]
    across = lax.broadcasted_iota(jnp.int32, (8, size), 1)
    down = lax.broadcasted_iota(jnp.int32, (8, size), 0)
    blocks = [a[8 * i : 8 * i + 8, :] for i in range(size // 8)]
    for k in range(len(blocks)):
        base = 8 * k
        panel = blocks[k]
        columns = [
            jnp.broadcast_to(panel[:, base + j : base + j + 1], (8, size)) for j in range(8)
        ]
        for j in range(8):
            pivot = 1.0 / columns[j][j : j + 1, :]
            lead = columns[j]
            for i in range(8):
                if i != j:
                    entry = columns[i][j : j + 1, :] * pivot
                    columns[i] = jnp.where(down == j, entry, columns[i] - lead * entry)
            columns[j] = jnp.where(down == j, pivot, -lead * pivot)
        inside = (across >= base) & (across < base + 8)
        panel = jnp.where(inside, jnp.where(across - base == down, 1.0, 0.0), panel)
        terms = [columns[j] * panel[j : j + 1, :] for j in range(8)]
        while len(terms) > 1:
            terms = [terms[i] + terms[i + 1] for i in range(0, len(terms), 2)]
        panel = terms[0]
        order = list(range(k + 1, len(blocks))) + list(range(k))
        for i in order:
            block = blocks[i]
            terms = [block[:, base + j : base + j + 1] * panel[j : j + 1, :] for j in range(8)]
            while len(terms) > 1:
                terms = [terms[m] + terms[m + 1] for m in range(0, len(terms), 2)]
            blocks[i] = jnp.where(inside, 0.0, block) - terms[0]
        blocks[k] = panel
    return jnp.concatenate(blocks, axis=0)


def solve_kernel(moments, scale, diagonal, out):
    size = moments.shape[0]
    half = size // 2
    cov = moments[:, :size] * scale[:, :size] + diagonal[...]
    right = moments[:, size:] * scale[:, size:]
    corner = invert(cov[:half, :half])
    cross = cov[:half, half:]
    across = mul(corner, cross)
    rest = invert(cov[half:, half:] - mul(cross.T, across))
    first = mul(corner, right[:half])
    second = mul(rest, right[half:] - mul(cross.T, first))
    out[half:] = second
    out[:half] = first - mul(across, second)


def solve_call(moments, scale, diagonal):
    vmem = pl.BlockSpec(memory_space=pltpu.VMEM)
    size = moments.shape[0]
    return pl.pallas_call(
        solve_kernel,
        out_shape=jax.ShapeDtypeStruct((size, moments.shape[1] - size), jnp.float32),
        in_specs=[vmem] * 3,
        out_specs=vmem,
        compiler_params=pltpu.CompilerParams(vmem_limit_bytes=32 * 2**20),
        name="gain",
    )(moments, scale, diagonal)


def local(ensemble, obs_values, obs_noise, obs_var, obs_offset, owner):
    rows, width = ensemble.shape
    n_ens = lax.axis_size("ens")
    n_state = lax.axis_size("state")
    members = width * n_ens
    states = rows * n_state
    reach = states // 4
    size = obs_offset.shape[1]
    here = lax.axis_index("state")
    positions = here * rows + jnp.arange(rows, dtype=jnp.int32)
    places = owner[:, None] * rows + obs_offset

    masked = jnp.where(
        jnp.repeat(here == owner, size)[:, None],
        jnp.take(ensemble, obs_offset.reshape(-1), axis=0),
        0.0,
    )
    noise_sums = jnp.sum(obs_noise[: NB - 1].astype(jnp.float32), axis=2).reshape(-1)
    sums = jnp.concatenate([jnp.sum(masked, axis=1), jnp.where(here == 0, noise_sums, 0.0)])
    prior, totals = spread_call(n_state, n_ens, masked, jnp.broadcast_to(sums, (8,) + sums.shape))
    means = totals[0] / members
    noise_means = means[NB * size :].reshape(NB - 1, size)
    means = means[: NB * size].reshape(NB, size)
    current = jnp.concatenate([prior, ensemble], axis=0)
    aims = jnp.concatenate([places.reshape(-1), positions])
    for batch in range(NB):
        scale = cycle_taper(places[batch][:, None], aims[None, :], states, reach) / (members - 1)
        variance = obs_var[batch]
        prior, current, aims = current[:size], current[size:], aims[size:]
        anom = prior - means[0][:, None]
        spread = jnp.einsum("pm,qm->pq", anom, anom, precision=finest)
        cross = jnp.einsum("pm,sm->ps", anom, current, precision=finest)
        moments = sum_call(n_ens, jnp.concatenate([spread, cross], axis=1), 1 + batch)
        gain = solve_call(moments, scale, jnp.diag(variance))
        misfit = (
            obs_values[batch][:, None]
            + jnp.sqrt(variance)[:, None] * obs_noise[batch].astype(jnp.float32)
            - prior
        )
        current = current + jnp.einsum(
            "ps,pm->sm", gain, misfit, precision=lax.Precision.HIGH
        )
        if batch + 1 < NB:
            misfit_mean = obs_values[batch] + jnp.sqrt(variance) * noise_means[batch] - means[0]
            later = gain[:, : (NB - 1 - batch) * size]
            means = means[1:] + jnp.einsum(
                "ps,p->s", later, misfit_mean, precision=finest
            ).reshape(-1, size)
    return current


def solution(mesh):
    in_specs = (P("state", "ens"), P(), P(None, None, "ens"), P(), P(), P())
    out_specs = P("state", "ens")
    return jax.shard_map(local, mesh=mesh, in_specs=in_specs, out_specs=out_specs, check_vma=False)
```
